32 devices in a mesh: zs: 4 (over z), ys: 8 (over y, x, core).
Axes of the slice: x: 2, y: 2, z: 4, core: 2. Of those that a mesh axis runs over, the one named last changes fastest.
Arguments:
- polarization: bfloat16 [2, 6, 256, 128, 512], P(None, None, None, 'ys', 'zs'), may hold values from -6 to 6
- theta_index: int32 [512], replicated, may hold values from 0 to 179
- phi_index: int32 [512], replicated, may hold values from 0 to 359
Outputs:
- mueller: float32 [16, 512], replicated
The draws below stay inside these ranges and needn't reach their ends.
All inputs are finite; a program needn't handle non-finite values.
Results may differ from the reference program's by a relative error of at most 0.0033.
Values sent between devices are 32-bit elements.
A program may use at most 64 MiB of HBM per device.

```python
import math
import jax
import jax.numpy as jnp
from jax import lax

GX = 256
DIRS = 512
NTHETA = 180
NPHI = 360
NY = 128
NZ = 512


def with_ends(result, rng, least, largest):
    place = [jax.random.randint(jax.random.fold_in(rng, axis), (), 0, length) for axis, length in enumerate(result.shape)]
    longest = result.shape.index(max(result.shape))
    beside = place[:longest] + [(place[longest] + 1) % result.shape[longest]] + place[longest + 1:]
    return result.at[tuple(place)].set(least).at[tuple(beside)].set(largest)


def block_scale(rng, dims, split, smallest, high):
    def one(axis_at, shards_of):
        heights = jax.random.uniform(jax.random.fold_in(jax.random.fold_in(rng, 6), axis_at), (shards_of,), jnp.float32, smallest / len(split), high / len(split))
        return jnp.repeat(jnp.exp(heights), dims[axis_at] // shards_of).reshape((-1,) + (1,) * (len(dims) - axis_at - 1))

    gain = one(*split[0])
    for cut in split[1:]:
        gain = gain * one(*cut)
    return gain


def centred(own_key, dims, spread, limit, cuts=(), dtype=jnp.bfloat16):
    result = jax.random.normal(own_key, dims, jnp.float32) * spread
    if len(cuts) > 0:
        result = block_scale(own_key, dims, cuts, -0.22, 0.18) * result
    return jnp.clip(result, min=-limit, max=limit).astype(dtype)


def setup_inputs(seed: int = 0) -> dict:
    key_list = jax.random.split(jax.random.key(seed), 4)
    return {
        "polarization": centred(key_list[0], (2, 6, GX, NY, NZ), 1.0, 6.0, ((3, 8), (4, 4))),
        "theta_index": with_ends(jax.random.randint(key_list[1], (DIRS,), 0, NTHETA), jax.random.fold_in(key_list[1], 1), 0, NTHETA - 1).astype(jnp.int32),
        "phi_index": with_ends(jax.random.randint(key_list[2], (DIRS,), 0, NPHI), jax.random.fold_in(key_list[2], 1), 0, NPHI - 1).astype(jnp.int32),
    }


wave_step = 0.6
pauli_set = (((1, 0), (0, 1)), ((1, 0), (0, -1)), ((0, 1), (1, 0)), ((0, -1j), (1j, 0)))

def angles(theta_index, phi_index):
    polar_angle = math.pi * (theta_index.astype(jnp.float32) + 0.5) / NTHETA
    azimuth = 2.0 * math.pi * phi_index.astype(jnp.float32) / NPHI
    return (polar_angle, azimuth)

def mueller_of(amplitude, polar_angle, azimuth):
    unit_theta = (jnp.cos(polar_angle) * jnp.cos(azimuth), jnp.cos(polar_angle) * jnp.sin(azimuth), -jnp.sin(polar_angle))
    unit_phi = (-jnp.sin(azimuth), jnp.cos(azimuth))
    real_jones = [[None, None], [None, None]]
    imag_jones = [[None, None], [None, None]]
    for s, unit_vec in enumerate((unit_theta, unit_phi)):
        for p in range(2):
            real_sum = 0.0
            imag_sum = 0.0
            for c in range(len(unit_vec)):
                real_sum = real_sum + unit_vec[c] * amplitude[:, 3 * p + c]
                imag_sum = imag_sum + unit_vec[c] * amplitude[:, 6 + 3 * p + c]
            real_jones[s][p] = real_sum
            imag_jones[s][p] = imag_sum
    elements = []
    for i in range(4):
        for j in range(4):
            summed = 0.0
            for a in range(2):
                for b in range(2):
                    for c in range(2):
                        for e in range(2):
                            weight = complex(pauli_set[i][a][b]) * complex(pauli_set[j][c][e])
                            if weight == 0:
                                continue
                            z_real = real_jones[b][c] * real_jones[a][e] + imag_jones[b][c] * imag_jones[a][e]
                            z_imag = imag_jones[b][c] * real_jones[a][e] - real_jones[b][c] * imag_jones[a][e]
                            summed = summed + weight.real * z_real - weight.imag * z_imag
            elements.append(0.5 * summed)
    return jnp.stack(elements)

def reference(polarization, theta_index, phi_index):
    halves, components, cells_x, total_y, total_z = polarization.shape
    polar_angle, azimuth = angles(theta_index, phi_index)
    unit_x = jnp.sin(polar_angle) * jnp.cos(azimuth)
    unit_y = jnp.sin(polar_angle) * jnp.sin(azimuth)
    unit_z = jnp.cos(polar_angle)
    pos_x = (jnp.arange(cells_x) - cells_x // 2).astype(jnp.float32)
    pos_y = (jnp.arange(total_y) - total_y // 2).astype(jnp.float32)
    pos_z = (jnp.arange(total_z) - total_z // 2).astype(jnp.float32)
    flattened = polarization.astype(jnp.float32).reshape(halves, components, cells_x, total_y * total_z)
    scaling = 1.0 / math.sqrt(cells_x * total_y * total_z)
    block_size = 8

    def one_block(first_row):
        bx = lax.dynamic_slice_in_dim(unit_x, first_row, block_size)
        by = lax.dynamic_slice_in_dim(unit_y, first_row, block_size)
        bz = lax.dynamic_slice_in_dim(unit_z, first_row, block_size)
        phase_x = wave_step * bx[:, None] * pos_x[None, :]
        tables = jnp.stack([jnp.cos(phase_x), jnp.sin(phase_x)]).astype(jnp.bfloat16)
        summed = jnp.einsum('tdx,rcxq->tdrcq', tables.astype(jnp.float32), flattened, precision=lax.Precision.HIGHEST)
        real_x = summed[0, :, 0] + summed[1, :, 1]
        imag_x = summed[0, :, 1] - summed[1, :, 0]
        phase_yz = wave_step * (by[:, None, None] * pos_y[None, :, None] + bz[:, None, None] * pos_z[None, None, :])
        phase_yz = phase_yz.reshape(block_size, total_y * total_z)
        cos_yz = jnp.cos(phase_yz)[:, None, :]
        sin_yz = jnp.sin(phase_yz)[:, None, :]
        real_part = lax.optimization_barrier(jnp.sum(real_x * cos_yz + imag_x * sin_yz, axis=-1))
        imag_part = lax.optimization_barrier(jnp.sum(imag_x * cos_yz - real_x * sin_yz, axis=-1))
        return jnp.concatenate([real_part, imag_part], axis=1) * scaling
    firsts = (jnp.arange(DIRS // block_size) * block_size).astype(jnp.int32)
    amplitude = lax.map(one_block, firsts).reshape(DIRS, 12)
    return mueller_of(amplitude, polar_angle, azimuth)
```

```python
import functools
import math

import jax
import jax.numpy as jnp
from jax import lax
from jax.experimental import pallas as pl
from jax.experimental.pallas import tpu as pltpu
from jax.sharding import PartitionSpec as P

NTHETA = 180
NPHI = 360
MESH = pl.DeviceIdType.MESH

wave_step = 0.6
pauli_set = (((1, 0), (0, 1)), ((1, 0), (0, -1)), ((0, 1), (1, 0)), ((0, -1j), (1j, 0)))


def angles(theta_index, phi_index):
    polar_angle = math.pi * (theta_index.astype(jnp.float32) + 0.5) / NTHETA
    azimuth = 2.0 * math.pi * phi_index.astype(jnp.float32) / NPHI
    return (polar_angle, azimuth)


def mueller_rows(real_jones, imag_jones):
    rows = []
    for i in range(4):
        for j in range(4):
            summed = 0.0
            for a in range(2):
                for b in range(2):
                    for c in range(2):
                        for e in range(2):
                            weight = complex(pauli_set[i][a][b]) * complex(pauli_set[j][c][e])
                            if weight == 0:
                                continue
                            if weight.real != 0:
                                z_real = (
                                    real_jones[b][c] * real_jones[a][e]
                                    + imag_jones[b][c] * imag_jones[a][e]
                                )
                                summed = summed + weight.real * z_real
                            else:
                                z_imag = (
                                    imag_jones[b][c] * real_jones[a][e]
                                    - real_jones[b][c] * imag_jones[a][e]
                                )
                                summed = summed - weight.imag * z_imag
            rows.append(0.5 * summed)
    return rows


def transform_kernel(pol, cos_x, sin_x, cos_y, sin_y, cos_a, sin_a, out, table, data):
    cells_x, cells_y, cells_z = pol.shape[2:]
    depth = cells_x * cells_y
    width = cos_y.shape[1]
    block = 2 * width

    @pl.when(pl.program_id(0) == 0)
    def build():
        cy = jnp.concatenate([cos_y[...]] * 2, axis=1)
        sy = jnp.concatenate([sin_y[...]] * 2, axis=1)
        for first in range(0, depth, block):
            row = lax.broadcasted_iota(jnp.int32, (cells_x, block), 0)
            column = lax.broadcasted_iota(jnp.int32, (cells_x, block), 1)
            low = (row - first // cells_y) * cells_y
            spread = jnp.where((column >= low) & (column < low + cells_y), 1.0, 0.0).astype(
                jnp.bfloat16
            )
            cx = jnp.dot(cos_x[...], spread, preferred_element_type=jnp.float32)
            sx = jnp.dot(sin_x[...], spread, preferred_element_type=jnp.float32)
            table[:, first : first + block] = (cx * cy - sx * sy).astype(jnp.bfloat16)
            table[:, depth + first : depth + first + block] = (sx * cy + cx * sy).astype(
                jnp.bfloat16
            )

    real = pol[0, 0].reshape(depth, cells_z)
    imag = pol[1, 0].reshape(depth, cells_z)
    data[:depth, :cells_z] = real
    data[depth:, :cells_z] = imag
    data[:depth, cells_z:] = imag
    data[depth:, cells_z:] = -real
    summed = jnp.dot(table[...], data[...], preferred_element_type=jnp.float32)
    g_real = summed[:, :cells_z]
    g_imag = summed[:, cells_z:]
    ca = cos_a[...]
    sa = sin_a[...]
    f_real = g_real * ca + g_imag * sa
    f_imag = g_imag * ca - g_real * sa
    out[0, 0:1, :] = jnp.sum(f_real.T, axis=0, keepdims=True)
    out[0, 1:2, :] = jnp.sum(f_imag.T, axis=0, keepdims=True)


def reduce_kernel(axes, counts, scaling, amp, unit, out, first_buf, second_buf, *sems):
    place = {name: lax.axis_index(name) for name in axes}

    def other(name, step):
        ids = dict(place)
        ids[name] = lax.rem(place[name] + step, counts[name])
        return tuple(ids[n] for n in axes)

    barrier = pltpu.get_barrier_semaphore()
    total = 0
    for name in axes:
        for step in range(1, counts[name]):
            pl.semaphore_signal(barrier, inc=1, device_id=other(name, step), device_id_type=MESH)
            total += 1

    rows = []
    for half in range(2):
        for s in range(2):
            for p in range(2):
                summed = 0.0
                for c in range(3 - s):
                    summed = summed + unit[3 * s + c : 3 * s + c + 1, :] * amp[
                        3 * p + c, half : half + 1, :
                    ]
                rows.append(summed * scaling)
    local = jnp.concatenate(rows, axis=0)
    pl.semaphore_wait(barrier, total)

    for stage, (name, buf) in enumerate(zip(reversed(axes), (first_buf, second_buf))):
        send, recv = sems[2 * stage], sems[2 * stage + 1]
        me = place[name]
        buf[me] = local
        copies = []
        for step in range(1, counts[name]):
            copy = pltpu.make_async_remote_copy(
                src_ref=buf.at[me],
                dst_ref=buf.at[me],
                send_sem=send.at[step],
                recv_sem=recv.at[step],
                device_id=other(name, step),
                device_id_type=MESH,
            )
            copy.start()
            copies.append(copy)
        for copy in copies:
            copy.wait()
        local = buf[0]
        for slot in range(1, counts[name]):
            local = local + buf[slot]

    def entry(half, s, p):
        at = 4 * half + 2 * s + p
        return local[at : at + 1, :]

    real_jones = [[entry(0, s, p) for p in range(2)] for s in range(2)]
    imag_jones = [[entry(1, s, p) for p in range(2)] for s in range(2)]
    for at, row in enumerate(mueller_rows(real_jones, imag_jones)):
        out[at : at + 1, :] = row


def body(axes, counts, polarization, theta_index, phi_index):
    halves, components, cells_x, cells_y, cells_z = polarization.shape
    total_y = cells_y * counts["ys"]
    total_z = cells_z * counts["zs"]
    directions = theta_index.shape[0]
    polar_angle, azimuth = angles(theta_index, phi_index)
    sin_t, cos_t = jnp.sin(polar_angle), jnp.cos(polar_angle)
    sin_p, cos_p = jnp.sin(azimuth), jnp.cos(azimuth)
    unit_x = sin_t * cos_p
    unit_y = sin_t * sin_p
    unit_z = cos_t
    scaling = 1.0 / math.sqrt(cells_x * total_y * total_z)

    pos_x = (jnp.arange(cells_x) - cells_x // 2).astype(jnp.float32)
    phase_x = wave_step * unit_x[:, None] * pos_x[None, :]
    cos_x = jnp.cos(phase_x).astype(jnp.bfloat16)
    sin_x = jnp.sin(phase_x).astype(jnp.bfloat16)

    lanes = 128
    centre_y = 0.5 * (cells_y - 1)
    pos_y = (jnp.arange(lanes) % cells_y).astype(jnp.float32) - centre_y
    phase_y = wave_step * unit_y[:, None] * pos_y[None, :]
    offset_y = (lax.axis_index("ys") * cells_y - total_y // 2).astype(jnp.float32) + centre_y
    pos_z = (lax.axis_index("zs") * cells_z + jnp.arange(cells_z) - total_z // 2).astype(
        jnp.float32
    )
    phase_a = wave_step * (unit_y[:, None] * offset_y + unit_z[:, None] * pos_z[None, :])
    depth = cells_x * cells_y

    def whole(array):
        return pl.BlockSpec(array.shape, lambda c: (0, 0))

    small = (cos_x, sin_x, jnp.cos(phase_y), jnp.sin(phase_y), jnp.cos(phase_a), jnp.sin(phase_a))
    amp = pl.pallas_call(
        transform_kernel,
        grid=(components,),
        out_shape=jax.ShapeDtypeStruct((components, 8, directions), jnp.float32),
        in_specs=[
            pl.BlockSpec((halves, 1, cells_x, cells_y, cells_z), lambda c: (0, c, 0, 0, 0))
        ]
        + [whole(array) for array in small],
        out_specs=pl.BlockSpec((1, 8, directions), lambda c: (c, 0, 0)),
        scratch_shapes=[
            pltpu.VMEM((directions, 2 * depth), jnp.bfloat16),
            pltpu.VMEM((2 * depth, 2 * cells_z), jnp.bfloat16),
        ],
        compiler_params=pltpu.CompilerParams(dimension_semantics=("arbitrary",)),
    )(polarization, *small)

    zero = jnp.zeros_like(sin_t)
    unit = jnp.stack([cos_t * cos_p, cos_t * sin_p, -sin_t, -sin_p, cos_p, zero, zero, zero])
    first, second = reversed(axes)
    return pl.pallas_call(
        functools.partial(reduce_kernel, axes, counts, scaling),
        out_shape=jax.ShapeDtypeStruct((16, directions), jnp.float32),
        in_specs=[pl.BlockSpec(memory_space=pltpu.VMEM)] * 2,
        out_specs=pl.BlockSpec(memory_space=pltpu.VMEM),
        scratch_shapes=[
            pltpu.VMEM((counts[first], 8, directions), jnp.float32),
            pltpu.VMEM((counts[second], 8, directions), jnp.float32),
            pltpu.SemaphoreType.DMA((counts[first],)),
            pltpu.SemaphoreType.DMA((counts[first],)),
            pltpu.SemaphoreType.DMA((counts[second],)),
            pltpu.SemaphoreType.DMA((counts[second],)),
        ],
        compiler_params=pltpu.CompilerParams(collective_id=0, has_side_effects=True),
    )(amp, unit)


def solution(mesh):
    axes = tuple(mesh.axis_names)
    counts = dict(mesh.shape)
    return jax.shard_map(
        functools.partial(body, axes, counts),
        mesh=mesh,
        in_specs=(P(None, None, None, "ys", "zs"), P(), P()),
        out_specs=P(),
        check_vma=False,
    )
```
